32 devices in a mesh: dp: 2 (over y), expert: 16 (over z, x, core).
Axes of the slice: x: 2, y: 2, z: 4, core: 2. Of those that a mesh axis runs over, the one named last changes fastest.
Arguments:
- tokens: bfloat16 [2048, 2560], P(('dp', 'expert')), may hold values from -6 to 6
- expert_ids: int32 [2048, 6], P(('dp', 'expert')), may hold values from 0 to 15, all different within a row; in each aligned block of 64 rows (0 to 63, 64 to 127, ...) at most 32 rows name the same one
- gate_scores: float32 [2048, 6], P(('dp', 'expert')), may hold values from 0.02 to 0.4
- w_gate: bfloat16 [16, 2560, 768], P('expert', 'dp'), may hold values from -0.125 to 0.125
- w_up: bfloat16 [16, 2560, 768], P('expert', 'dp'), may hold values from -0.125 to 0.125
- w_down: bfloat16 [16, 768, 2560], P('expert', None, 'dp'), may hold values from -0.21875 to 0.21875
Outputs:
- mixed: bfloat16 [2048, 2560], P(('dp', 'expert'))
- expert_load: int32 [16], P('expert')
- balance_loss: float32 [], replicated
The draws below stay inside these ranges and needn't reach their ends.
Inputs may be any that keep to these rules, and one draw needn't show every extreme that they name: `expert_ids`: each row names 6 different experts. The rows of one device name any one expert at most 32 times, and in every draw some device names some expert exactly 32 times.
All inputs are finite; a program needn't handle non-finite values.
Results may differ from the reference program's by a relative error of at most 0.0085.
Values may be sent and summed in bfloat16 or wider, within the bound.
No kernel may reach another device: no remote copies, remote signals or barrier semaphores. Data moves between devices by JAX's collectives and lax.ppermute only.
A program may use at most 64 MiB of HBM per device.

```python
import math
import jax
import jax.numpy as jnp
import numpy as np
from jax import lax

D = 2560
HID = 768
TOPK = 6
TOK_DEV = 64
EXPERTS = 16
CAP = 32
TOKENS = 2048


def block_levels(stream_key, shape, pieces, smallest, largest):
    gain, own = 1.0, jax.random.fold_in(stream_key, 6)
    for dim, blocks in pieces:
        draws = jnp.exp(jax.random.uniform(jax.random.fold_in(own, dim), (blocks,), jnp.float32, smallest / len(pieces), largest / len(pieces)))
        gain = gain * jnp.repeat(draws, shape[dim] // blocks).reshape([-1 if axis == dim else 1 for axis in range(len(shape))])
    return gain


def routed_block(rng, own, number, rows, amount, top, reach, lean):
    sequence = jax.random.permutation(rng, amount)
    heavy_load, common = shares(amount, rows * top, reach, lean, True), shares(amount, rows * top, reach, lean, False)
    places = jnp.arange(amount)

    def named(lengths, offset_by):
        used = int((lengths > 0).sum())
        fixed = max(1, used // 4)
        passed = fixed + (places - fixed + offset_by * (used - fixed)) % max(1, amount - fixed)
        return jnp.zeros((amount,), jnp.int32).at[sequence[jnp.where(places < fixed, places, passed)]].set(jnp.asarray(lengths, jnp.int32))

    lengths = jnp.where(number % 4 == 0, named(heavy_load, number // 4), named(common, number - number // 4 - 1))
    mixed = jax.random.permutation(jax.random.fold_in(own, 3), amount)
    giver, sink = mixed[0:amount // 2 * 2:2], mixed[1:amount // 2 * 2:2]
    room = jnp.minimum(lengths[giver] - 1, reach - lengths[sink]) // 2
    room = jnp.where((giver == sequence[0]) | (sink == sequence[0]) | (lengths[sink] == 0), 0, jnp.maximum(room, 0))
    passed = jax.random.randint(jax.random.fold_in(own, 4), (amount // 2,), 0, 1 << 20) % (room + 1)
    lengths = lengths.at[giver].add(-passed).at[sink].add(passed)
    labels = jnp.searchsorted(jnp.cumsum(lengths), jnp.arange(rows * top), side="right").astype(jnp.int32)
    table = labels.reshape(top, rows).T
    table = table[jax.random.permutation(jax.random.fold_in(own, 1), rows)]
    offset_by = jax.random.randint(jax.random.fold_in(own, 2), (rows, 1), 0, top)
    return jnp.take_along_axis(table, (jnp.arange(top)[None, :] + offset_by) % top, axis=1)


def shares(number_of, total, bound, lean, full):
    portions = [(1 << 20) // math.isqrt(rank ** lean) + 1 for rank in range(1, number_of + 1)]
    largest = bound if full else min(bound, max(-(-total // number_of), total * portions[0] // sum(portions)))
    least = 1 if total - largest >= number_of - 1 else 0
    holding, spare = [largest] + [least] * (number_of - 1), total - largest - least * (number_of - 1)
    while spare > 0:
        movable = [i for i in range(1, number_of) if holding[i] < largest] or [i for i in range(1, number_of) if holding[i] < bound]
        pool, remaining = sum([portions[i] for i in movable]), spare
        for i in movable:
            addition = min(bound - holding[i], max(1, remaining * portions[i] // pool), spare)
            holding[i] = holding[i] + addition
            spare = spare - addition
    return np.array(holding)


def bell_draw(rng, dims, scale, bound, shards=(), kind=jnp.bfloat16):
    entries = scale * jax.random.normal(rng, dims, jnp.float32)
    if shards:
        entries = entries * block_levels(rng, dims, shards, -0.22, 0.18)
    return jnp.clip(entries, -bound, bound).astype(kind)


def setup_inputs(seed: int = 0) -> dict:
    key_list = jax.random.split(jax.random.key(seed), 7)
    tokens = bell_draw(key_list[0], (TOKENS, D), 1.0, 6.0, ((0, 32),))
    expert_ids_keys = jax.random.split(jax.random.fold_in(key_list[1], 1), TOKENS // TOK_DEV)
    expert_ids_turns = jax.random.permutation(jax.random.fold_in(key_list[1], 3), TOKENS // TOK_DEV)
    expert_ids = jax.vmap(lambda own, number: routed_block(jax.random.fold_in(key_list[1], 2), own, number, TOK_DEV, EXPERTS, TOPK, CAP, 2))(expert_ids_keys, expert_ids_turns).reshape((TOKENS, TOPK))
    gate_scores = jnp.clip(jnp.exp(math.log(0.4) - 2.9957323 * jax.random.uniform(key_list[2], (TOKENS, TOPK), jnp.float32) ** block_levels(key_list[2], (TOKENS, TOPK), ((0, 32),), -0.2, 0.2)), 0.02, 0.4)
    w_gate = bell_draw(key_list[3], (EXPERTS, D, HID), D ** -0.5, 0.125, ((0, 16), (1, 2)))
    w_up = bell_draw(key_list[4], (EXPERTS, D, HID), D ** -0.5, 0.125, ((0, 16), (1, 2)))
    w_down = bell_draw(key_list[5], (EXPERTS, HID, D), HID ** -0.5, 0.21875, ((0, 16), (2, 2)))
    return {"tokens": tokens, "expert_ids": expert_ids, "gate_scores": gate_scores, "w_gate": w_gate, "w_up": w_up, "w_down": w_down}


def reference(tokens, expert_ids, gate_scores, w_gate, w_up, w_down):
    total, width = tokens.shape
    experts = w_gate.shape[0]
    blocks = total // TOK_DEV
    pairs = TOK_DEV * TOPK
    block_ids = expert_ids.reshape(blocks, pairs)
    onehot = (block_ids[:, :, None] == jnp.arange(experts, dtype=jnp.int32)[None, None, :]).astype(jnp.int32)
    ranks = jnp.cumsum(onehot, axis=1) - onehot
    slot_of = jnp.sum(ranks * onehot, axis=2).astype(jnp.int32)
    block_of = jnp.broadcast_to(jnp.arange(blocks, dtype=jnp.int32)[:, None], (blocks, pairs))
    token_of = block_of * TOK_DEV + (jnp.arange(pairs, dtype=jnp.int32) // TOPK)[None, :]
    table = jnp.full((experts, blocks, CAP), -1, jnp.int32)
    table = table.at[block_ids, block_of, slot_of].set(token_of)
    slot_tok = slot_of.reshape(total, TOPK)
    row_base = (jnp.arange(total, dtype=jnp.int32) // TOK_DEV) * CAP

    def per_expert(carry, inputs):
        index, gate_w, up_w, down_w, sources = inputs
        live = sources >= 0
        rows = jnp.where(live[:, None], tokens[jnp.maximum(sources, 0)], jnp.zeros((), tokens.dtype))
        gate = jnp.dot(rows, gate_w, preferred_element_type=jnp.float32)
        up = jnp.dot(rows, up_w, preferred_element_type=jnp.float32)
        hidden = (jax.nn.silu(gate) * up).astype(jnp.bfloat16)
        produced = jnp.dot(hidden, down_w, preferred_element_type=jnp.float32).astype(jnp.bfloat16)
        match = expert_ids == index
        weight = jnp.sum(jnp.where(match, gate_scores, jnp.zeros((), gate_scores.dtype)), axis=1)
        slot = jnp.sum(jnp.where(match, slot_tok, 0), axis=1).astype(jnp.int32)
        picked = produced[row_base + slot].astype(jnp.float32)
        return carry + weight[:, None] * picked, None

    mixed, _ = lax.scan(per_expert, jnp.zeros((total, width), jnp.float32),
                        (jnp.arange(experts, dtype=jnp.int32), w_gate, w_up, w_down,
                         table.reshape(experts, blocks * CAP)))
    load = jnp.sum(onehot, axis=(0, 1)).astype(jnp.int32)
    mass = jnp.sum(onehot.astype(jnp.float32) * gate_scores.reshape(blocks, pairs)[:, :, None], axis=(0, 1))
    load_f = load.astype(jnp.float32)
    balance_loss = jnp.sum((experts * load_f / (TOPK * total)) * (mass / total))
    return mixed.astype(jnp.bfloat16), load, balance_loss
```

```python
import jax
import jax.numpy as jnp
from jax import lax
from jax.sharding import PartitionSpec as P

BF16 = jnp.bfloat16
F32 = jnp.float32


def dot(a, b, dims):
    return lax.dot_general(a, b, dims, preferred_element_type=F32)


def swap(value, axis, bit):
    size = lax.axis_size(axis)
    return lax.ppermute(value, axis, [(i, i ^ bit) for i in range(size)])


def exchange(parts):
    groups = lax.axis_size("dp")
    if groups == 1:
        return parts
    if groups == 2:
        return [parts[0], swap(parts[1], "dp", 1)]
    got = lax.all_to_all(jnp.stack(parts), "dp", split_axis=0, concat_axis=0, tiled=True)
    return [got[g] for g in range(groups)]


def split_width(value):
    groups = lax.axis_size("dp")
    width = value.shape[-1] // groups
    parts = [value[..., g * width : (g + 1) * width] for g in range(groups)]
    if groups == 2:
        first = lax.axis_index("dp") == 0
        return [jnp.where(first, parts[0], parts[1]), jnp.where(first, parts[1], parts[0])]
    return parts


def join_width(parts):
    if len(parts) == 2:
        first = lax.axis_index("dp") == 0
        parts = [jnp.where(first, parts[0], parts[1]), jnp.where(first, parts[1], parts[0])]
    return jnp.concatenate(parts, axis=-1)


def routing(expert_ids, gate_scores, experts):
    rows = expert_ids.shape[0]
    hit = expert_ids[:, :, None] == jnp.arange(experts, dtype=jnp.int32)[None, None, :]
    chosen = jnp.any(hit, axis=1)
    gate = jnp.sum(jnp.where(hit, gate_scores[:, :, None], 0.0), axis=1)
    order = jnp.arange(rows, dtype=jnp.int32)
    earlier = (order[None, :] < order[:, None]).astype(BF16)
    slot = dot(earlier, chosen.astype(BF16), (((1,), (0,)), ((), ())))
    code = jnp.where(chosen, slot, -1.0)
    high = gate.astype(BF16)
    low = (gate - high.astype(F32)).astype(BF16)
    table = jnp.concatenate([code.astype(BF16), high, low], axis=1)
    pad = -table.shape[1] % 128
    return jnp.pad(table, ((0, 0), (0, pad)))


def tree_sum(values):
    while values.shape[0] > 1:
        half = values.shape[0] // 2
        values = values[:half] + values[half:]
    return values[0]


def on_device(tokens, expert_ids, gate_scores, w_gate, w_up, w_down):
    tok_rows, full = tokens.shape
    topk = expert_ids.shape[1]
    experts = lax.axis_size("expert")
    groups = lax.axis_size("dp")
    width = full // groups
    hid = w_gate.shape[2]
    capacity = 4 * tok_rows * topk // (3 * experts)
    me = lax.axis_index("expert")
    w_first = jnp.concatenate([w_gate[0], w_up[0]], axis=1)
    w_last = w_down[0]

    table = routing(expert_ids, gate_scores, experts)
    sent = [jnp.concatenate([part, table], axis=1) for part in split_width(tokens)]
    base = jnp.stack(exchange(sent))
    cols = base.shape[2] - width
    picks = (
        jnp.arange(cols, dtype=jnp.int32)[None, :]
        == (jnp.arange(3, dtype=jnp.int32) * experts + me)[:, None]
    ).astype(BF16)
    slots = jnp.arange(capacity, dtype=jnp.int32).astype(F32)

    far = list(range(4, experts, 4))
    moved_far = {j: swap(base, "expert", j) for j in far}
    chunks = {}
    beside = swap(base, "expert", 2)
    chunks["side"] = [beside]
    for j in far:
        chunks[j] = [moved_far[j], swap(moved_far[j], "expert", 2)]
    chunks["home"] = [base]

    stats = {}
    acc = None
    for name, own in chunks.items():
        mine = jnp.stack(own, axis=1)
        theirs = swap(mine, "expert", 1)
        block = jnp.stack([mine, theirs], axis=1)
        n = 2 * len(own)
        block = block.reshape(groups, n, tok_rows, width + cols)
        notes = block[..., width:]
        got = dot(notes, picks, (((3,), (1,)), ((), ())))
        got = jnp.moveaxis(got, 3, 0)
        place = got[0][:, :, None, :] == slots[None, None, :, None]
        rows = dot(
            place.astype(BF16), block[..., :width], (((3,), (2,)), ((0, 1), (0, 1)))
        ).astype(BF16)
        rows = rows.reshape(groups, n * capacity, width)
        part = dot(rows, w_first, (((2,), (0,)), ((), ())))
        traded = exchange([part[0]] + [part[g].astype(BF16) for g in range(1, groups)])
        total = sum(x.astype(F32) for x in traded)
        hidden = (jax.nn.silu(total[:, :hid]) * total[:, hid:]).astype(BF16)
        all_hidden = jnp.stack(exchange([hidden] * groups))
        produced = dot(all_hidden, w_last, (((2,), (0,)), ((), ()))).astype(BF16)
        produced = produced.reshape(groups, n, capacity, width)
        high = jnp.where(place, got[1][:, :, None, :], 0.0).astype(BF16)
        low = jnp.where(place, got[2][:, :, None, :], 0.0).astype(BF16)
        back = (((2,), (2,)), ((0, 1), (0, 1)))
        mixed = dot(high, produced, back) + dot(low, produced, back)
        half = n // 2
        mixed = mixed[:, :half] + swap(mixed[:, half:].astype(BF16), "expert", 1).astype(F32)
        if half == 2:
            mixed = mixed[:, 0] + swap(mixed[:, 1].astype(BF16), "expert", 2).astype(F32)
        else:
            mixed = mixed[:, 0]
        if name == "side":
            mixed = swap(mixed.astype(BF16), "expert", 2).astype(F32)
        elif name != "home":
            mixed = swap(mixed.astype(BF16), "expert", name).astype(F32)
        acc = mixed if acc is None else acc + mixed
        codes = notes[..., :experts].astype(F32)
        load = jnp.sum((codes >= 0).astype(F32), axis=2)
        mass = jnp.sum(
            notes[..., experts : 2 * experts].astype(F32)
            + notes[..., 2 * experts : 3 * experts].astype(F32),
            axis=2,
        )
        pair = jnp.stack([load, mass], axis=2)
        stats[name] = pair.reshape(groups, 2, len(own), 2, experts)

    near = jnp.concatenate([stats["home"], stats["side"]], axis=2)
    planes = jnp.stack([near] + [stats[j] for j in far])
    planes = tree_sum(planes)
    planes = tree_sum(planes)
    planes = tree_sum(planes)
    planes = tree_sum(planes)
    load, mass = planes[0], planes[1]

    done = exchange([acc[0]] + [acc[g].astype(BF16) for g in range(1, groups)])
    mixed = join_width([x.astype(BF16) for x in done])

    tokens_all = tok_rows * groups * experts
    term = experts * load / (topk * tokens_all) * (mass / tokens_all)
    balance_loss = jnp.sum(term)
    expert_load = jnp.sum(
        jnp.where(jnp.arange(experts, dtype=jnp.int32) == me, load, 0.0), keepdims=True
    ).astype(jnp.int32)
    return (mixed, expert_load, balance_loss)


def solution(mesh):
    in_specs = (
        P(("dp", "expert"), None),
        P(("dp", "expert"), None),
        P(("dp", "expert"), None),
        P("expert", "dp", None),
        P("expert", "dp", None),
        P("expert", None, "dp"),
    )
    out_specs = (P(("dp", "expert"), None), P("expert"), P())
    return jax.shard_map(
        on_device, mesh=mesh, in_specs=in_specs, out_specs=out_specs, check_vma=False
    )
```
